32 devices in a mesh: dp: 4 (over y, core), pipe: 4 (over z), tensor: 2 (over x).
Axes of the slice: x: 2, y: 2, z: 4, core: 2. Of those that a mesh axis runs over, the one named last changes fastest.
Arguments:
- section_in: bfloat16 [4, 1024, 8192], P('pipe', 'tensor', 'dp'), may hold values from -6 to 6
- norm_gain: float32 [4, 8192], P('pipe', 'dp'), may hold values from 0.5 to 2
- w_query: bfloat16 [4, 8192, 4096], P('pipe', 'dp', 'tensor')
- key_value_weight: bfloat16 [4, 8192, 4, 256], P('pipe', 'dp', 'tensor')
- w_out: bfloat16 [4, 4096, 8192], P('pipe', 'tensor', 'dp'), may hold values from -0.09375 to 0.09375
Outputs:
- section_out: bfloat16 [4, 1024, 8192], P('pipe', 'tensor', 'dp')
The draws below stay inside these ranges and needn't reach their ends.
All inputs are finite; a program needn't handle non-finite values.
Results may differ from the reference program's by a relative error of at most 0.034.
Values may be sent and summed in bfloat16 or wider, within the bound.
A program may use at most 64 MiB of HBM per device.

```python
import math
import jax
import jax.numpy as jnp
from jax import lax

MODEL_WIDTH = 8192
QUERY_HEAD_COUNT = 32
KEY_VALUE_HEADS = 4
HEAD_SIZE = 128
SECTION_TOKENS = 1024
RELAY_SECTIONS = 4
N_DP = 4
N_TENSOR = 2


def query_weight_matrix(key):
    inner_product = jax.random.fold_in(key, 101)
    return jax.random.truncated_normal(inner_product, -4.0, 4.0, (RELAY_SECTIONS, MODEL_WIDTH, QUERY_HEAD_COUNT * HEAD_SIZE), jnp.float32) * MODEL_WIDTH ** (-0.5)


def draw_w_query(key, part):
    return query_weight_matrix(key).astype(jnp.bfloat16)


def draw_key_value_weight(key, part):
    inner_product = jax.random.fold_in(key, 202)
    own_section = jax.random.truncated_normal(inner_product, -4.0, 4.0, (RELAY_SECTIONS, MODEL_WIDTH, KEY_VALUE_HEADS, 2 * HEAD_SIZE), jnp.float32) * MODEL_WIDTH ** (-0.5)
    return own_section.astype(jnp.bfloat16)


def block_scale(key, extent, cuts, low, top_value):
    level, own = 1.0, jax.random.fold_in(key, 6)
    for position, shards_of in cuts:
        draws = jnp.exp(jax.random.uniform(jax.random.fold_in(own, position), (shards_of,), jnp.float32, low / len(cuts), top_value / len(cuts)))
        level = level * jnp.repeat(draws, extent[position] // shards_of).reshape([-1 if axis == position else 1 for axis in range(len(extent))])
    return level


def centred(stream_key, dims, width, bound, split=(), kind=jnp.bfloat16):
    values = jax.random.normal(stream_key, dims, jnp.float32) * width
    if len(split) > 0:
        values = block_scale(stream_key, dims, split, -0.22, 0.18) * values
    return jnp.clip(values, min=-bound, max=bound).astype(kind)


def setup_inputs(seed: int = 0) -> dict:
    splits = jax.random.split(jax.random.key(seed), 6)
    return {
        "section_in": centred(splits[0], (RELAY_SECTIONS, SECTION_TOKENS, MODEL_WIDTH), 1.0, 6.0, ((0, 4), (1, 2), (2, 4))),
        "norm_gain": jnp.clip(jnp.exp(math.log(2.0) - 1.3862944 * jax.random.uniform(splits[1], (RELAY_SECTIONS, MODEL_WIDTH), jnp.float32) ** block_scale(splits[1], (RELAY_SECTIONS, MODEL_WIDTH), ((0, 4), (1, 4)), -0.2, 0.2)), 0.5, 2.0),
        "w_query": draw_w_query(jax.random.fold_in(splits[5], 71), 0),
        "key_value_weight": draw_key_value_weight(jax.random.fold_in(splits[5], 71), 0),
        "w_out": centred(splits[4], (RELAY_SECTIONS, QUERY_HEAD_COUNT * HEAD_SIZE, MODEL_WIDTH), (QUERY_HEAD_COUNT * HEAD_SIZE) ** -0.5, 0.09375, ((0, 4), (1, 2), (2, 4))),
    }


eps = 1e-05
rope_base = 500000.0

def rope_tables(positions, head_dim):
    half = head_dim // 2
    freqs = rope_base ** (-(jnp.arange(half).astype(jnp.float32) * 2.0) / head_dim)
    angle = positions[:, None] * freqs[None, :]
    return (jnp.cos(angle), jnp.sin(angle))

def rotate(field, cosine, sine):
    half = field.shape[-1] // 2
    first = field[..., :half]
    second = field[..., half:]
    return jnp.concatenate([first * cosine - second * sine, second * cosine + first * sine], axis=-1)

def softmax_rows(scores, allowed):
    scores = jnp.where(allowed, scores, -jnp.inf)
    top = lax.optimization_barrier(jnp.max(scores, axis=-1, keepdims=True))
    expo = jnp.exp(scores - top)
    return (expo / lax.optimization_barrier(jnp.sum(expo, axis=-1, keepdims=True))).astype(jnp.bfloat16)

def one_section(arrived, gain, w_query, key_value_weight, w_out):
    wide = arrived.astype(jnp.float32)
    square_sum = lax.optimization_barrier(jnp.sum(wide * wide, axis=1))
    row_norm_scale = lax.rsqrt(square_sum / MODEL_WIDTH + eps)
    normed_input = (wide * gain[None, :]).astype(jnp.bfloat16)
    block_width = MODEL_WIDTH // N_DP

    def query_block(index, total):
        first = (index * block_width).astype(jnp.int32)
        columns = lax.dynamic_slice_in_dim(normed_input, first, block_width, 1)
        weights_rows = lax.dynamic_slice_in_dim(w_query, first, block_width, 0)
        rounded = jnp.dot(columns, weights_rows, preferred_element_type=jnp.float32).astype(jnp.bfloat16)
        return total + lax.optimization_barrier(rounded).astype(jnp.float32)
    query_sum = lax.fori_loop(0, N_DP, query_block, jnp.zeros((SECTION_TOKENS, QUERY_HEAD_COUNT * HEAD_SIZE), jnp.float32))
    rotary_pairs = jnp.dot(normed_input, key_value_weight.reshape(MODEL_WIDTH, KEY_VALUE_HEADS * 2 * HEAD_SIZE), preferred_element_type=jnp.float32)
    rotary_pairs = rotary_pairs.reshape(SECTION_TOKENS, KEY_VALUE_HEADS, 2 * HEAD_SIZE) * row_norm_scale[:, None, None]
    positions = jnp.arange(SECTION_TOKENS).astype(jnp.float32)
    cosine, sine = rope_tables(positions, HEAD_SIZE)
    query = rotate(query_sum.reshape(SECTION_TOKENS, QUERY_HEAD_COUNT, HEAD_SIZE) * row_norm_scale[:, None, None], cosine[:, None, :], sine[:, None, :]).astype(jnp.bfloat16)
    keys = rotate(rotary_pairs[..., :HEAD_SIZE], cosine[:, None, :], sine[:, None, :]).astype(jnp.bfloat16)
    values = rotary_pairs[..., HEAD_SIZE:].astype(jnp.bfloat16)
    allowed = positions[None, :] <= positions[:, None]
    head_group = QUERY_HEAD_COUNT // KEY_VALUE_HEADS

    def one_head(head):
        query_head = lax.dynamic_index_in_dim(query, head, 1, keepdims=False)
        key_head = lax.dynamic_index_in_dim(keys, head // head_group, 1, keepdims=False)
        value_head = lax.dynamic_index_in_dim(values, head // head_group, 1, keepdims=False)
        scores = jnp.dot(query_head, key_head.T, preferred_element_type=jnp.float32) * HEAD_SIZE ** (-0.5)
        weights = softmax_rows(scores, allowed)
        return jnp.dot(weights, value_head, preferred_element_type=jnp.float32).astype(jnp.bfloat16)
    heads_out = lax.map(one_head, jnp.arange(QUERY_HEAD_COUNT).astype(jnp.int32))
    w_heads = w_out.reshape(QUERY_HEAD_COUNT, HEAD_SIZE, MODEL_WIDTH)
    per_group = QUERY_HEAD_COUNT // N_TENSOR

    def out_block(index, total):
        first = (index * per_group).astype(jnp.int32)
        outs_group = lax.dynamic_slice_in_dim(heads_out, first, per_group, 0).astype(jnp.float32)
        weights_group = lax.dynamic_slice_in_dim(w_heads, first, per_group, 0).astype(jnp.float32)
        rounded = jnp.einsum('hsd,hdc->sc', outs_group, weights_group).astype(jnp.bfloat16)
        return total + lax.optimization_barrier(rounded).astype(jnp.float32)
    projected = lax.fori_loop(0, N_TENSOR, out_block, jnp.zeros((SECTION_TOKENS, MODEL_WIDTH), jnp.float32))
    return (wide + projected).astype(jnp.bfloat16)

def reference(section_in, norm_gain, w_query, key_value_weight, w_out):
    arrived = jnp.roll(section_in, 1, axis=0)
    return lax.map(lambda items: one_section(*items), (arrived, norm_gain, w_query, key_value_weight, w_out))
```

```python
import functools

import jax
import jax.numpy as jnp
from jax import lax
from jax.experimental import pallas as pl
from jax.experimental.pallas import tpu as pltpu
from jax.sharding import PartitionSpec as P

MODEL_WIDTH = 8192
QUERY_HEAD_COUNT = 32
KEY_VALUE_HEADS = 4


eps = 1e-05
rope_base = 500000.0


def shifted(block, axis, distance):
    devices = range(lax.axis_size(axis))
    route = [((i - distance) % len(devices), i) for i in devices]
    return lax.ppermute(block, axis, route)


def rope_tables(positions, head_dim):
    half = head_dim // 2
    freqs = rope_base ** (-(jnp.arange(half).astype(jnp.float32) * 2.0) / head_dim)
    angle = positions[:, None] * freqs[None, :]
    return (jnp.cos(angle), jnp.sin(angle))


def rotate(field, cosine, sine):
    half = field.shape[-1] // 2
    first = field[..., :half]
    second = field[..., half:]
    return jnp.concatenate(
        [first * cosine - second * sine, second * cosine + first * sine], axis=-1
    )


def softmax_rows(scores, allowed):
    scores = jnp.where(allowed, scores, -jnp.inf)
    top = jnp.max(scores, axis=-1, keepdims=True)
    expo = jnp.exp(scores - top)
    return (expo / jnp.sum(expo, axis=-1, keepdims=True)).astype(jnp.bfloat16)


def per_device(section_in, norm_gain, w_query, key_value_weight, w_out):
    resident = section_in[0]
    arrived = shifted(resident, "pipe", 1)
    gathered = lax.all_gather(arrived, "tensor", axis=0, tiled=True)
    seq_len = gathered.shape[0]
    width = gathered.shape[1]
    head_dim = key_value_weight.shape[3] // 2
    pair_heads = key_value_weight.shape[2]
    query_heads = w_query.shape[2] // head_dim
    groups = lax.axis_size("dp")
    member = lax.axis_index("dp")
    head_group = QUERY_HEAD_COUNT // KEY_VALUE_HEADS
    score_scale = head_dim ** (-0.5)
    wide = gathered.astype(jnp.float32)
    square_part = jnp.sum(wide * wide, axis=1)
    normed_input = (wide * norm_gain[0][None, :]).astype(jnp.bfloat16)
    pair_terms = jnp.dot(
        normed_input,
        key_value_weight[0].reshape(width, pair_heads * 2 * head_dim),
        preferred_element_type=jnp.float32,
    )
    local_rows = seq_len // groups
    first_row = member * local_rows
    positions = jnp.arange(seq_len).astype(jnp.float32)
    cosine, sine = rope_tables(positions, head_dim)
    own_cosine = lax.dynamic_slice_in_dim(cosine, first_row, local_rows, 0)
    own_sine = lax.dynamic_slice_in_dim(sine, first_row, local_rows, 0)
    own_places = lax.dynamic_slice_in_dim(positions, first_row, local_rows, 0)
    pair_share, square_share = (
        lax.psum_scatter(pair_terms, "dp", scatter_dimension=0, tiled=True),
        lax.psum_scatter(square_part, "dp", scatter_dimension=0, tiled=True),
    )
    own_scale = lax.rsqrt(square_share / MODEL_WIDTH + eps)
    pair_share = pair_share.reshape(local_rows, pair_heads, 2 * head_dim) * own_scale[:, None, None]
    own_keys = rotate(
        pair_share[..., :head_dim], own_cosine[:, None, :], own_sine[:, None, :]
    ).astype(jnp.bfloat16)
    own_values = pair_share[..., head_dim:].astype(jnp.bfloat16)
    keys, values = (
        lax.all_gather(own_keys, "dp", axis=0, tiled=True),
        lax.all_gather(own_values, "dp", axis=0, tiled=True),
    )
    w_heads = w_out[0].reshape(query_heads, head_dim, width)
    w_flat = w_query[0]
    query_sum = lax.psum_scatter(
        jnp.dot(normed_input, w_flat, preferred_element_type=jnp.float32).astype(jnp.bfloat16),
        "dp",
        scatter_dimension=0,
        tiled=True,
    ).astype(jnp.float32)
    query = rotate(
        query_sum.reshape(local_rows, query_heads, head_dim) * own_scale[:, None, None],
        own_cosine[:, None, :],
        own_sine[:, None, :],
    ).astype(jnp.bfloat16)
    allowed = positions[None, :] <= own_places[:, None]

    def attend_group(number):
        query_group = lax.dynamic_slice_in_dim(query, number * head_group, head_group, 1)
        key_head = lax.dynamic_index_in_dim(keys, number, 1, keepdims=False)
        value_head = lax.dynamic_index_in_dim(values, number, 1, keepdims=False)
        scores = (
            jnp.einsum("rgd,sd->grs", query_group, key_head, preferred_element_type=jnp.float32)
            * score_scale
        )
        weights = softmax_rows(scores, allowed[None])
        return jnp.einsum(
            "grs,sd->grd", weights, value_head, preferred_element_type=jnp.float32
        ).astype(jnp.bfloat16)

    row_results = lax.map(attend_group, jnp.arange(pair_heads))
    row_results = row_results.reshape(query_heads, local_rows, head_dim)
    contrib = jnp.einsum(
        "hsd,hdc->sc",
        lax.all_gather(row_results, "dp", axis=1, tiled=True),
        w_heads,
        preferred_element_type=jnp.float32,
    )
    summed = lax.psum_scatter(
        contrib.astype(jnp.bfloat16), "tensor", scatter_dimension=0, tiled=True
    ).astype(jnp.float32)
    result = (arrived.astype(jnp.float32) + summed).astype(jnp.bfloat16)
    return result[None]

MESH = pl.DeviceIdType.MESH
BF16 = jnp.bfloat16
F32 = jnp.float32
PIECES = 8
ATT_ROWS = 128


def relay_kernel(
    pipe_size,
    x_hbm,
    gain_ref,
    wq_hbm,
    wkv_hbm,
    wo_hbm,
    cos_ref,
    sin_ref,
    out_hbm,
    arrived,
    w_all,
    w_out,
    normed,
    squares,
    first_send,
    first_recv,
    keep,
    second_send,
    second_recv,
    keep_two,
    query,
    pair_buf,
    keys,
    values,
    heads,
    part_send,
    part_recv,
    own_part,
    result,
    load_sem,
    z_sem,
    x_sem,
    first_sem,
    second_sem,
    pair_sem,
    near_sem,
    far_sem,
    pass_sem,
    part_sem,
    store_sem,
):
    p = lax.axis_index("pipe")
    t = lax.axis_index("tensor")
    d = lax.axis_index("dp")
    c = d % 2
    y = d // 2
    nxt = {"pipe": (p + 1) % pipe_size}
    prev = {"pipe": (p + pipe_size - 1) % pipe_size}
    side = {"tensor": 1 - t}
    core = {"dp": d + 1 - 2 * c}
    across = {"dp": (d + 2) % 4}
    half = arrived.shape[1]
    width = arrived.shape[2]
    rows = half // PIECES
    q_cols = wq_hbm.shape[1] // 4
    head = wkv_hbm.shape[1] // 4
    q_heads = q_cols // head
    steps = PIECES + 1
    chunks = 2 * half // ATT_ROWS
    half_chunks = chunks // 2

    def remote(src, dst, sem, k, where):
        return pltpu.make_async_remote_copy(
            src_ref=src,
            dst_ref=dst,
            send_sem=sem.at[0, k],
            recv_sem=sem.at[1, k],
            device_id=where,
            device_id_type=MESH,
        )

    barrier = pltpu.get_barrier_semaphore()
    for where in (nxt, prev, side, core, across):
        pl.semaphore_signal(barrier, inc=1, device_id=where, device_id_type=MESH)
    pl.semaphore_wait(barrier, 5)

    def z_copy(k):
        span = pl.ds(k * rows, rows)
        return remote(x_hbm.at[0, span], arrived.at[t, span], z_sem, k, nxt)

    def x_copy(k):
        span = pl.ds(k * rows, rows)
        return remote(arrived.at[t, span], arrived.at[t, span], x_sem, k, side)

    def x_landed(k):
        span = pl.ds(k * rows, rows)
        return remote(arrived.at[1 - t, span], arrived.at[1 - t, span], x_sem, k, side)

    def first_copy(k):
        return remote(first_send.at[k], first_recv.at[k], first_sem, k, core)

    def second_copy(k):
        return remote(second_send.at[k], second_recv.at[k], second_sem, k, across)

    def pair_copy(k, slot):
        return remote(pair_buf.at[slot, k], pair_buf.at[slot, k], pair_sem, k, core)

    def block(k, owner):
        return heads.at[k, :, pl.ds(pl.multiple_of(owner * q_cols, q_cols), q_cols)]

    far_owner = (d + 2) % 4

    def near_copy(k):
        return remote(block(k, d), block(k, d), near_sem, k, core)

    def far_copy(k):
        return remote(block(k, d), block(k, d), far_sem, k, across)

    def pass_copy(k):
        return remote(block(k, far_owner), block(k, far_owner), pass_sem, k, core)

    def part_copy(k):
        return remote(part_send.at[k], part_recv.at[k], part_sem, k, side)

    def start_z(k, carry):
        z_copy(k).start()
        return carry

    lax.fori_loop(0, PIECES, start_z, 0)

    loads = []
    for b in range(4):
        loads.append(
            pltpu.make_async_copy(
                wq_hbm.at[:, b * q_cols : (b + 1) * q_cols],
                w_all.at[b, :, 0:q_cols],
                load_sem.at[2 * b],
            )
        )
        loads.append(
            pltpu.make_async_copy(
                wkv_hbm.at[:, b * head : (b + 1) * head],
                w_all.at[b, :, q_cols : q_cols + head],
                load_sem.at[2 * b + 1],
            )
        )
    out_load = pltpu.make_async_copy(wo_hbm, w_out, load_sem.at[8])
    for load in loads:
        load.start()
    out_load.start()
    normed[...] = jnp.zeros_like(normed)
    squares[...] = jnp.zeros_like(squares)
    for load in loads:
        load.wait()

    def prepare(side_index, piece, base):
        wide = arrived[side_index, pl.ds(piece * rows, rows), :].astype(F32)
        normed[base : base + rows, :] = (wide * gain_ref[...]).astype(BF16)
        total = wide[:, 0:head] * wide[:, 0:head]
        for k in range(1, width // head):
            cut = wide[:, k * head : (k + 1) * head]
            total = total + cut * cut
        squares[base : base + rows, :] = total

    def project(s):
        for other in range(2):
            index = 2 * other + (1 - c)
            first_send[s, other, :, 0 : q_cols + head] = jnp.dot(
                normed[...], w_all[index], preferred_element_type=F32
            ).astype(BF16)
            first_send[s, other, :, q_cols + head :] = squares[...].astype(BF16)
        first_copy(s).start()
        for other in range(2):
            index = 2 * other + c
            keep[s % 2, other, :, 0 : q_cols + head] = jnp.dot(
                normed[...], w_all[index], preferred_element_type=F32
            )
            keep[s % 2, other, :, q_cols + head :] = squares[...]

    def reduce_core(s):
        first_copy(s).wait_recv()
        second_send[s] = (keep[s % 2, 1 - y] + first_recv[s, 1 - y].astype(F32)).astype(BF16)
        second_copy(s).start()
        keep_two[s % 2] = keep[s % 2, y] + first_recv[s, y].astype(F32)

    is_value = c.astype(F32)

    def finish(s):
        second_copy(s).wait_recv()
        total = keep_two[s % 2] + second_recv[s].astype(F32)
        scale = lax.rsqrt(
            jnp.sum(total[:, q_cols + head :], axis=1, keepdims=True) / MODEL_WIDTH + eps
        )
        own_rows = pl.ds(pl.multiple_of(t * half + (s % PIECES) * rows, rows), rows)
        side_rows = pl.ds(
            pl.multiple_of((1 - t) * half + ((s + PIECES - 1) % PIECES) * rows, rows), rows
        )
        cosine = jnp.concatenate([cos_ref[own_rows, :], cos_ref[side_rows, :]], axis=0)
        sine = jnp.concatenate([sin_ref[own_rows, :], sin_ref[side_rows, :]], axis=0)
        turned = []
        for k in range(q_heads):
            v = total[:, k * head : (k + 1) * head] * scale
            turned.append((v * cosine + pltpu.roll(v, head // 2, 1) * sine).astype(BF16))

        @pl.when(s < PIECES)
        def _():
            for k in range(q_heads):
                query[own_rows, k * head : (k + 1) * head] = turned[k][:rows]

        @pl.when(s > 0)
        def _():
            for k in range(q_heads):
                query[side_rows, k * head : (k + 1) * head] = turned[k][rows:]

        v = total[:, q_cols : q_cols + head] * scale
        pair_cos = cosine * (1.0 - is_value) + is_value
        pair_sin = sine * (1.0 - is_value)
        pair_buf[c, s] = (v * pair_cos + pltpu.roll(v, head // 2, 1) * pair_sin).astype(BF16)
        pair_copy(s, c).start()

    def step(s, carry):
        @pl.when(s < PIECES)
        def _():
            z_copy(s).wait_recv()
            x_copy(s).start()
            prepare(t, s, 0)

        @pl.when((s > 0) & (s < steps))
        def _():
            x_landed(s - 1).wait_recv()
            prepare(1 - t, s - 1, rows)

        @pl.when(s < steps)
        def _():
            project(s)

        @pl.when((s > 0) & (s < steps + 1))
        def _():
            reduce_core(s - 1)

        @pl.when(s > 1)
        def _():
            finish(s - 2)

        return carry

    lax.fori_loop(0, steps + 2, step, 0)

    def land_pairs(k, carry):
        pair_copy(k, 1 - c).wait_recv()
        return carry

    lax.fori_loop(0, steps, land_pairs, 0)

    def place(k, carry):
        own = pl.ds(pl.multiple_of(t * half + k * rows, rows), rows)
        other = pl.ds(pl.multiple_of((1 - t) * half + k * rows, rows), rows)
        keys[own, :] = pair_buf[0, k, 0:rows, :]
        keys[other, :] = pair_buf[0, k + 1, rows:, :]
        values[own, :] = pair_buf[1, k, 0:rows, :]
        values[other, :] = pair_buf[1, k + 1, rows:, :]
        return carry

    lax.fori_loop(0, PIECES, place, 0)
    out_load.wait()
    factor = head ** (-0.5) * 1.4426950408889634

    def attend(i, first, count):
        at = lax.broadcasted_iota(jnp.int32, (ATT_ROWS, count), 0) + first
        seen = lax.broadcasted_iota(jnp.int32, (ATT_ROWS, count), 1) <= at
        for k in range(q_heads):
            q = query[pl.ds(first, ATT_ROWS), k * head : (k + 1) * head]
            scores = lax.dot_general(
                q, keys[0:count, :], (((1,), (1,)), ((), ())), preferred_element_type=F32
            )
            scores = jnp.where(seen, scores, -1e30)
            top = jnp.max(scores, axis=1, keepdims=True)
            expo = jnp.exp2((scores - top) * factor)
            total = jnp.sum(expo, axis=1, keepdims=True)
            mixed = jnp.dot(expo.astype(BF16), values[0:count, :], preferred_element_type=F32)
            spot = pl.ds(pl.multiple_of(d * q_cols + k * head, head), head)
            heads[i, :, spot] = (mixed / total).astype(BF16)

    def out_step(i, carry):
        @pl.when(i < chunks)
        def _():
            which = (1 - t + i // half_chunks) % 2
            first = pl.multiple_of(which * half + (i % half_chunks) * ATT_ROWS, ATT_ROWS)

            @pl.when(which == 0)
            def _():
                attend(i, first, half)

            @pl.when(which == 1)
            def _():
                attend(i, first, 2 * half)

            far_copy(i).start()
            near_copy(i).start()

        @pl.when((i > 0) & (i < chunks + 1))
        def _():
            far_landed(i - 1).wait_recv()
            pass_copy(i - 1).start()

        @pl.when(i > 1)
        def _():
            k = i - 2
            near_landed(k).wait_recv()
            pass_landed(k).wait_recv()

            @pl.when(k < half_chunks)
            def _():
                for n in range(4):
                    cut = slice(n * (width // 4), (n + 1) * (width // 4))
                    part_send[k, :, cut] = jnp.dot(
                        heads[k], w_out[:, cut], preferred_element_type=F32
                    ).astype(BF16)
                part_copy(k).start()

            @pl.when(k >= half_chunks)
            def _():
                for n in range(4):
                    cut = slice(n * (width // 4), (n + 1) * (width // 4))
                    own_part[k - half_chunks, :, cut] = jnp.dot(
                        heads[k], w_out[:, cut], preferred_element_type=F32
                    )

        return carry

    def far_landed(k):
        return remote(block(k, far_owner), block(k, far_owner), far_sem, k, across)

    def near_landed(k):
        owner = d + 1 - 2 * c
        return remote(block(k, owner), block(k, owner), near_sem, k, core)

    def pass_landed(k):
        owner = (d + 3 - 2 * c) % 4
        return remote(block(k, owner), block(k, owner), pass_sem, k, core)

    lax.fori_loop(0, chunks + 2, out_step, 0)

    def store(k):
        span = pl.ds(k * ATT_ROWS, ATT_ROWS)
        return pltpu.make_async_copy(result.at[k], out_hbm.at[0, span], store_sem.at[k])

    def close(k, carry):
        part_copy(k).wait_recv()
        span = pl.ds(pl.multiple_of(k * ATT_ROWS, ATT_ROWS), ATT_ROWS)
        result[k] = (
            arrived[t, span, :].astype(F32) + (own_part[k] + part_recv[k].astype(F32))
        ).astype(BF16)
        store(k).start()
        return carry

    lax.fori_loop(0, half_chunks, close, 0)

    def drain_pieces(k, carry):
        z_copy(k).wait_send()
        x_copy(k).wait_send()
        return carry

    def drain_steps(k, carry):
        first_copy(k).wait_send()
        second_copy(k).wait_send()
        pair_copy(k, c).wait_send()
        return carry

    def drain_chunks(k, carry):
        near_copy(k).wait_send()
        far_copy(k).wait_send()
        pass_copy(k).wait_send()
        return carry

    def drain_parts(k, carry):
        part_copy(k).wait_send()
        store(k).wait()
        return carry

    lax.fori_loop(0, PIECES, drain_pieces, 0)
    lax.fori_loop(0, steps, drain_steps, 0)
    lax.fori_loop(0, chunks, drain_chunks, 0)
    lax.fori_loop(0, half_chunks, drain_parts, 0)


def relay_device(pipe_size, section_in, norm_gain, w_query, key_value_weight, w_out):
    _, half, width = section_in.shape
    kv_cols = key_value_weight.shape[2] * key_value_weight.shape[3]
    head = key_value_weight.shape[3] // 2
    q_cols = w_query.shape[2] // 4
    cosine, sine = rope_tables(jnp.arange(2 * half).astype(F32), head)
    cosine = jnp.concatenate([cosine, cosine], axis=1)
    sine = jnp.concatenate([-sine, sine], axis=1)
    rows = half // PIECES
    steps = PIECES + 1
    message = q_cols + 2 * head
    chunks = 2 * half // ATT_ROWS
    vmem = pl.BlockSpec(memory_space=pltpu.VMEM)
    anywhere = pl.BlockSpec(memory_space=pl.ANY)
    dma = pltpu.SemaphoreType.DMA
    return pl.pallas_call(
        functools.partial(relay_kernel, pipe_size),
        out_shape=jax.ShapeDtypeStruct((1, half, width), BF16),
        in_specs=[anywhere, vmem, anywhere, anywhere, anywhere, vmem, vmem],
        out_specs=anywhere,
        scratch_shapes=[
            pltpu.VMEM((2, half, width), BF16),
            pltpu.VMEM((4, width, q_cols + head), BF16),
            pltpu.VMEM((4 * q_cols, width), BF16),
            pltpu.VMEM((2 * rows, width), BF16),
            pltpu.VMEM((2 * rows, head), F32),
            pltpu.VMEM((steps, 2, 2 * rows, message), BF16),
            pltpu.VMEM((steps, 2, 2 * rows, message), BF16),
            pltpu.VMEM((2, 2, 2 * rows, message), F32),
            pltpu.VMEM((steps, 2 * rows, message), BF16),
            pltpu.VMEM((steps, 2 * rows, message), BF16),
            pltpu.VMEM((2, 2 * rows, message), F32),
            pltpu.VMEM((2 * half, q_cols), BF16),
            pltpu.VMEM((2, steps, 2 * rows, head), BF16),
            pltpu.VMEM((2 * half, head), BF16),
            pltpu.VMEM((2 * half, head), BF16),
            pltpu.VMEM((chunks, ATT_ROWS, 4 * q_cols), BF16),
            pltpu.VMEM((chunks // 2, ATT_ROWS, width), BF16),
            pltpu.VMEM((chunks // 2, ATT_ROWS, width), BF16),
            pltpu.VMEM((chunks // 2, ATT_ROWS, width), F32),
            pltpu.VMEM((chunks // 2, ATT_ROWS, width), BF16),
            dma((9,)),
            dma((2, PIECES)),
            dma((2, PIECES)),
            dma((2, steps)),
            dma((2, steps)),
            dma((2, steps)),
            dma((2, chunks)),
            dma((2, chunks)),
            dma((2, chunks)),
            dma((2, chunks // 2)),
            dma((chunks // 2,)),
        ],
        compiler_params=pltpu.CompilerParams(
            collective_id=0, has_side_effects=True, vmem_limit_bytes=60 * 1024 * 1024
        ),
    )(
        section_in,
        norm_gain,
        w_query[0],
        key_value_weight[0].reshape(width, kv_cols),
        w_out[0],
        cosine,
        sine,
    )


def solution(mesh):
    fits = mesh.shape["dp"] == 4 and mesh.shape["tensor"] == 2 and mesh.shape["pipe"] > 2
    body = functools.partial(relay_device, mesh.shape["pipe"]) if fits else per_device
    return jax.shard_map(
        body,
        mesh=mesh,
        in_specs=(
            P("pipe", "tensor", "dp"),
            P("pipe", "dp"),
            P("pipe", "dp", "tensor"),
            P("pipe", "dp", "tensor", None),
            P("pipe", "tensor", "dp"),
        ),
        out_specs=P("pipe", "tensor", "dp"),
        check_vma=False,
    )
```

```python
import functools

import jax
import numpy as np
import jax.numpy as jnp
from jax import lax
from jax.experimental import pallas as pl
from jax.experimental.pallas import tpu as pltpu
from jax.sharding import PartitionSpec as P

MODEL_WIDTH = 8192
QUERY_HEAD_COUNT = 32
KEY_VALUE_HEADS = 4


eps = 1e-05
rope_base = 500000.0


def shifted(block, axis, distance):
    devices = range(lax.axis_size(axis))
    route = [((i - distance) % len(devices), i) for i in devices]
    return lax.ppermute(block, axis, route)


def rope_tables(positions, head_dim):
    half = head_dim // 2
    freqs = rope_base ** (-(jnp.arange(half).astype(jnp.float32) * 2.0) / head_dim)
    angle = positions[:, None] * freqs[None, :]
    return (jnp.cos(angle), jnp.sin(angle))


def rotate(field, cosine, sine):
    half = field.shape[-1] // 2
    first = field[..., :half]
    second = field[..., half:]
    return jnp.concatenate(
        [first * cosine - second * sine, second * cosine + first * sine], axis=-1
    )


def softmax_rows(scores, allowed):
    scores = jnp.where(allowed, scores, -jnp.inf)
    top = jnp.max(scores, axis=-1, keepdims=True)
    expo = jnp.exp(scores - top)
    return (expo / jnp.sum(expo, axis=-1, keepdims=True)).astype(jnp.bfloat16)


def per_device(section_in, norm_gain, w_query, key_value_weight, w_out):
    resident = section_in[0]
    arrived = shifted(resident, "pipe", 1)
    gathered = lax.all_gather(arrived, "tensor", axis=0, tiled=True)
    seq_len = gathered.shape[0]
    width = gathered.shape[1]
    head_dim = key_value_weight.shape[3] // 2
    pair_heads = key_value_weight.shape[2]
    query_heads = w_query.shape[2] // head_dim
    groups = lax.axis_size("dp")
    member = lax.axis_index("dp")
    head_group = QUERY_HEAD_COUNT // KEY_VALUE_HEADS
    score_scale = head_dim ** (-0.5)
    wide = gathered.astype(jnp.float32)
    square_part = jnp.sum(wide * wide, axis=1)
    normed_input = (wide * norm_gain[0][None, :]).astype(jnp.bfloat16)
    pair_terms = jnp.dot(
        normed_input,
        key_value_weight[0].reshape(width, pair_heads * 2 * head_dim),
        preferred_element_type=jnp.float32,
    )
    local_rows = seq_len // groups
    first_row = member * local_rows
    positions = jnp.arange(seq_len).astype(jnp.float32)
    cosine, sine = rope_tables(positions, head_dim)
    own_cosine = lax.dynamic_slice_in_dim(cosine, first_row, local_rows, 0)
    own_sine = lax.dynamic_slice_in_dim(sine, first_row, local_rows, 0)
    own_places = lax.dynamic_slice_in_dim(positions, first_row, local_rows, 0)
    pair_share, square_share = (
        lax.psum_scatter(pair_terms, "dp", scatter_dimension=0, tiled=True),
        lax.psum_scatter(square_part, "dp", scatter_dimension=0, tiled=True),
    )
    own_scale = lax.rsqrt(square_share / MODEL_WIDTH + eps)
    pair_share = pair_share.reshape(local_rows, pair_heads, 2 * head_dim) * own_scale[:, None, None]
    own_keys = rotate(
        pair_share[..., :head_dim], own_cosine[:, None, :], own_sine[:, None, :]
    ).astype(jnp.bfloat16)
    own_values = pair_share[..., head_dim:].astype(jnp.bfloat16)
    keys, values = (
        lax.all_gather(own_keys, "dp", axis=0, tiled=True),
        lax.all_gather(own_values, "dp", axis=0, tiled=True),
    )
    w_heads = w_out[0].reshape(query_heads, head_dim, width)
    w_flat = w_query[0]
    query_sum = lax.psum_scatter(
        jnp.dot(normed_input, w_flat, preferred_element_type=jnp.float32).astype(jnp.bfloat16),
        "dp",
        scatter_dimension=0,
        tiled=True,
    ).astype(jnp.float32)
    query = rotate(
        query_sum.reshape(local_rows, query_heads, head_dim) * own_scale[:, None, None],
        own_cosine[:, None, :],
        own_sine[:, None, :],
    ).astype(jnp.bfloat16)
    allowed = positions[None, :] <= own_places[:, None]

    def attend_group(number):
        query_group = lax.dynamic_slice_in_dim(query, number * head_group, head_group, 1)
        key_head = lax.dynamic_index_in_dim(keys, number, 1, keepdims=False)
        value_head = lax.dynamic_index_in_dim(values, number, 1, keepdims=False)
        scores = (
            jnp.einsum("rgd,sd->grs", query_group, key_head, preferred_element_type=jnp.float32)
            * score_scale
        )
        weights = softmax_rows(scores, allowed[None])
        return jnp.einsum(
            "grs,sd->grd", weights, value_head, preferred_element_type=jnp.float32
        ).astype(jnp.bfloat16)

    row_results = lax.map(attend_group, jnp.arange(pair_heads))
    row_results = row_results.reshape(query_heads, local_rows, head_dim)
    contrib = jnp.einsum(
        "hsd,hdc->sc",
        lax.all_gather(row_results, "dp", axis=1, tiled=True),
        w_heads,
        preferred_element_type=jnp.float32,
    )
    summed = lax.psum_scatter(
        contrib.astype(jnp.bfloat16), "tensor", scatter_dimension=0, tiled=True
    ).astype(jnp.float32)
    result = (arrived.astype(jnp.float32) + summed).astype(jnp.bfloat16)
    return result[None]

MESH = pl.DeviceIdType.MESH
BF16 = jnp.bfloat16
F32 = jnp.float32
PIECES = 8
ATT_ROWS = 64


def relay_kernel(
    pipe_size,
    x_hbm,
    gain_ref,
    wq_hbm,
    wkv_hbm,
    wo_hbm,
    cos_hbm,
    sin_hbm,
    out_ref,
    cos_ref,
    sin_ref,
    arrived,
    w_all,
    w_out,
    normed,
    squares,
    first_send,
    first_recv,
    keep,
    second_send,
    second_recv,
    keep_two,
    query,
    pair_buf,
    keys,
    values,
    heads,
    part_send,
    part_recv,
    own_part,
    load_sem,
    z_sem,
    x_sem,
    first_sem,
    second_sem,
    pair_sem,
    near_sem,
    far_sem,
    pass_sem,
    part_sem,
):
    p = lax.axis_index("pipe")
    t = lax.axis_index("tensor")
    d = lax.axis_index("dp")
    c = d % 2
    y = d // 2
    nxt = {"pipe": (p + 1) % pipe_size}
    prev = {"pipe": (p + pipe_size - 1) % pipe_size}
    side = {"tensor": 1 - t}
    core = {"dp": d + 1 - 2 * c}
    across = {"dp": (d + 2) % 4}
    half = arrived.shape[1]
    width = arrived.shape[2]
    rows = half // PIECES
    sub = rows // 2
    q_cols = wq_hbm.shape[1] // 4
    head = wkv_hbm.shape[1] // 4
    q_heads = q_cols // head
    steps = PIECES + 1
    chunks = 2 * half // ATT_ROWS
    half_chunks = chunks // 2

    def remote(src, dst, sem, k, where):
        return pltpu.make_async_remote_copy(
            src_ref=src,
            dst_ref=dst,
            send_sem=sem.at[0, k],
            recv_sem=sem.at[1, k],
            device_id=where,
            device_id_type=MESH,
        )

    barrier = pltpu.get_barrier_semaphore()
    for where in (nxt, prev, side, core, across):
        pl.semaphore_signal(barrier, inc=1, device_id=where, device_id_type=MESH)
    pl.semaphore_wait(barrier, 5)

    def z_copy(k):
        span = pl.ds(k * sub, sub)
        return remote(x_hbm.at[0, span], arrived.at[t, span], z_sem, k, nxt)

    def x_copy(k):
        span = pl.ds(k * sub, sub)
        return remote(arrived.at[t, span], arrived.at[t, span], x_sem, k, side)

    def x_landed(k):
        span = pl.ds(k * sub, sub)
        return remote(arrived.at[1 - t, span], arrived.at[1 - t, span], x_sem, k, side)

    late = pl.ds(rows, rows)

    def first_copy(k):
        return remote(first_send.at[k], first_recv.at[k], first_sem, k, core)

    def first_late(k):
        return remote(
            first_send.at[k, :, late], first_recv.at[k, :, late], first_sem, k, core
        )

    def second_copy(k):
        return remote(second_send.at[k], second_recv.at[k], second_sem, k, across)

    def second_late(k):
        return remote(
            second_send.at[k, late], second_recv.at[k, late], second_sem, k, across
        )

    def pair_copy(k, slot):
        return remote(pair_buf.at[slot, k], pair_buf.at[slot, k], pair_sem, k, core)

    def pair_late(k, slot):
        return remote(
            pair_buf.at[slot, k, late], pair_buf.at[slot, k, late], pair_sem, k, core
        )

    def by_step(k, whole, part, act):
        @pl.when(k < PIECES)
        def _():
            act(whole)

        @pl.when(k >= PIECES)
        def _():
            act(part)

    def block(k, owner):
        return heads.at[k, :, pl.ds(pl.multiple_of(owner * q_cols, q_cols), q_cols)]

    far_owner = (d + 2) % 4

    def near_copy(k):
        return remote(block(k, d), block(k, d), near_sem, k, core)

    def far_copy(k):
        return remote(block(k, d), block(k, d), far_sem, k, across)

    def pass_copy(k):
        return remote(block(k, far_owner), block(k, far_owner), pass_sem, k, core)

    def part_copy(k):
        return remote(part_send.at[k], part_recv.at[k], part_sem, k, side)

    def start_z(k, carry):
        z_copy(k).start()
        return carry

    lax.fori_loop(0, 2 * PIECES, start_z, 0)

    loads = []
    for b in range(4):
        loads.append(
            pltpu.make_async_copy(
                wq_hbm.at[:, b * q_cols : (b + 1) * q_cols],
                w_all.at[b, :, 0:q_cols],
                load_sem.at[2 * b],
            )
        )
        loads.append(
            pltpu.make_async_copy(
                wkv_hbm.at[:, b * head : (b + 1) * head],
                w_all.at[b, :, q_cols : q_cols + head],
                load_sem.at[2 * b + 1],
            )
        )
    loads.append(pltpu.make_async_copy(cos_hbm, cos_ref, load_sem.at[9]))
    loads.append(pltpu.make_async_copy(sin_hbm, sin_ref, load_sem.at[10]))
    out_load = pltpu.make_async_copy(wo_hbm, w_out, load_sem.at[8])
    for load in loads:
        load.start()
    out_load.start()
    z_copy(0).wait_recv()
    x_copy(0).start()
    normed[...] = jnp.zeros_like(normed)
    squares[...] = jnp.zeros_like(squares)
    for load in loads:
        load.wait()

    def prepare(side_index, piece, base):
        wide = arrived[side_index, pl.ds(piece * rows, rows), :].astype(F32)
        normed[base : base + rows, :] = (wide * gain_ref[...]).astype(BF16)
        total = wide[:, 0:head] * wide[:, 0:head]
        for k in range(1, width // head):
            cut = wide[:, k * head : (k + 1) * head]
            total = total + cut * cut
        squares[base : base + rows, :] = total

    def project(s):
        for other in range(2):
            index = 2 * other + (1 - c)
            first_send[s, other, :, 0 : q_cols + head] = jnp.dot(
                normed[...], w_all[index], preferred_element_type=F32
            ).astype(BF16)
            first_send[s, other, :, q_cols + head :] = squares[...].astype(BF16)
        by_step(s, first_copy, first_late, lambda make: make(s).start())

        @pl.when(s + 1 < PIECES)
        def _():
            z_copy(2 * s + 2).wait_recv()
            x_copy(2 * s + 2).start()

        for other in range(2):
            index = 2 * other + c
            keep[s % 2, other, :, 0 : q_cols + head] = jnp.dot(
                normed[...], w_all[index], preferred_element_type=F32
            )
            keep[s % 2, other, :, q_cols + head :] = squares[...]

    def reduce_core(s):
        by_step(s, first_copy, first_late, lambda make: make(s).wait_recv())
        second_send[s] = (keep[s % 2, 1 - y] + first_recv[s, 1 - y].astype(F32)).astype(BF16)
        by_step(s, second_copy, second_late, lambda make: make(s).start())
        keep_two[s % 2] = keep[s % 2, y] + first_recv[s, y].astype(F32)

    is_value = c.astype(F32)

    def finish(s):
        by_step(s, second_copy, second_late, lambda make: make(s).wait_recv())
        total = keep_two[s % 2] + second_recv[s].astype(F32)
        scale = lax.rsqrt(
            jnp.sum(total[:, q_cols + head :], axis=1, keepdims=True) / MODEL_WIDTH + eps
        )
        own_rows = pl.ds(pl.multiple_of(t * half + (s % PIECES) * rows, rows), rows)
        side_rows = pl.ds(
            pl.multiple_of((1 - t) * half + ((s + PIECES - 1) % PIECES) * rows, rows), rows
        )
        cosine = jnp.concatenate([cos_ref[own_rows, :], cos_ref[side_rows, :]], axis=0)
        sine = jnp.concatenate([sin_ref[own_rows, :], sin_ref[side_rows, :]], axis=0)
        turned = []
        for k in range(q_heads):
            v = total[:, k * head : (k + 1) * head] * scale
            turned.append((v * cosine + pltpu.roll(v, head // 2, 1) * sine).astype(BF16))

        @pl.when(s < PIECES)
        def _():
            for k in range(q_heads):
                query[own_rows, k * head : (k + 1) * head] = turned[k][:rows]

        @pl.when(s > 0)
        def _():
            for k in range(q_heads):
                query[side_rows, k * head : (k + 1) * head] = turned[k][rows:]

        v = total[:, q_cols : q_cols + head] * scale
        pair_cos = cosine * (1.0 - is_value) + is_value
        pair_sin = sine * (1.0 - is_value)
        pair_buf[c, s] = (v * pair_cos + pltpu.roll(v, head // 2, 1) * pair_sin).astype(BF16)
        by_step(s, pair_copy, pair_late, lambda make: make(s, c).start())

    def step(s, carry):
        @pl.when(s < PIECES)
        def _():
            z_copy(2 * s + 1).wait_recv()
            x_copy(2 * s + 1).start()
            prepare(t, s, 0)

        @pl.when((s > 0) & (s < steps))
        def _():
            x_landed(2 * s - 2).wait_recv()
            x_landed(2 * s - 1).wait_recv()
            prepare(1 - t, s - 1, rows)

        @pl.when(s < steps)
        def _():
            project(s)

        @pl.when((s > 0) & (s < steps + 1))
        def _():
            reduce_core(s - 1)

        @pl.when(s > 1)
        def _():
            finish(s - 2)

        return carry

    lax.fori_loop(0, steps + 2, step, 0)

    def land_pairs(k, carry):
        pair_copy(k, 1 - c).wait_recv()
        return carry

    lax.fori_loop(0, PIECES, land_pairs, 0)
    pair_late(PIECES, 1 - c).wait_recv()

    def place(k, carry):
        own = pl.ds(pl.multiple_of(t * half + k * rows, rows), rows)
        other = pl.ds(pl.multiple_of((1 - t) * half + k * rows, rows), rows)
        keys[own, :] = pair_buf[0, k, 0:rows, :]
        keys[other, :] = pair_buf[0, k + 1, rows:, :]
        values[own, :] = pair_buf[1, k, 0:rows, :]
        values[other, :] = pair_buf[1, k + 1, rows:, :]
        return carry

    lax.fori_loop(0, PIECES, place, 0)
    out_load.wait()
    factor = head ** (-0.5) * 1.4426950408889634

    def attend(i, first, count):
        at = lax.broadcasted_iota(jnp.int32, (ATT_ROWS, count), 0) + first
        seen = lax.broadcasted_iota(jnp.int32, (ATT_ROWS, count), 1) <= at
        for k in range(q_heads):
            q = query[pl.ds(first, ATT_ROWS), k * head : (k + 1) * head]
            scores = lax.dot_general(
                q, keys[0:count, :], (((1,), (1,)), ((), ())), preferred_element_type=F32
            )
            scores = jnp.where(seen, scores, -1e30)
            top = jnp.max(scores, axis=1, keepdims=True)
            expo = jnp.exp2((scores - top) * factor)
            total = jnp.sum(expo, axis=1, keepdims=True)
            mixed = jnp.dot(expo.astype(BF16), values[0:count, :], preferred_element_type=F32)
            spot = pl.ds(pl.multiple_of(d * q_cols + k * head, head), head)
            heads[i, :, spot] = (mixed / total).astype(BF16)

    def out_step(i, carry):
        @pl.when(i < chunks)
        def _():
            which = (1 - t + i // half_chunks) % 2
            first = pl.multiple_of(which * half + (i % half_chunks) * ATT_ROWS, ATT_ROWS)

            @pl.when(which == 0)
            def _():
                attend(i, first, half)

            @pl.when(which == 1)
            def _():
                attend(i, first, 2 * half)

            far_copy(i).start()
            near_copy(i).start()

        @pl.when((i > 0) & (i < chunks + 1))
        def _():
            far_landed(i - 1).wait_recv()
            pass_copy(i - 1).start()

        @pl.when(i > 1)
        def _():
            k = i - 2
            near_landed(k).wait_recv()
            pass_landed(k).wait_recv()

            @pl.when(k < half_chunks)
            def _():
                for n in range(4):
                    cut = slice(n * (width // 4), (n + 1) * (width // 4))
                    part_send[k, :, cut] = jnp.dot(
                        heads[k], w_out[:, cut], preferred_element_type=F32
                    ).astype(BF16)
                part_copy(k).start()

            @pl.when(k >= half_chunks)
            def _():
                for n in range(4):
                    cut = slice(n * (width // 4), (n + 1) * (width // 4))
                    own_part[k - half_chunks, :, cut] = jnp.dot(
                        heads[k], w_out[:, cut], preferred_element_type=F32
                    )

        return carry

    def far_landed(k):
        return remote(block(k, far_owner), block(k, far_owner), far_sem, k, across)

    def near_landed(k):
        owner = d + 1 - 2 * c
        return remote(block(k, owner), block(k, owner), near_sem, k, core)

    def pass_landed(k):
        owner = (d + 3 - 2 * c) % 4
        return remote(block(k, owner), block(k, owner), pass_sem, k, core)

    lax.fori_loop(0, chunks + 2, out_step, 0)

    def close(k, carry):
        part_copy(k).wait_recv()
        span = pl.ds(pl.multiple_of(k * ATT_ROWS, ATT_ROWS), ATT_ROWS)
        out_ref[0, span, :] = (
            arrived[t, span, :].astype(F32) + (own_part[k] + part_recv[k].astype(F32))
        ).astype(BF16)
        return carry

    lax.fori_loop(0, half_chunks, close, 0)

    def drain_pieces(k, carry):
        z_copy(k).wait_send()
        x_copy(k).wait_send()
        return carry

    def drain_steps(k, carry):
        first_copy(k).wait_send()
        second_copy(k).wait_send()
        pair_copy(k, c).wait_send()
        return carry

    def drain_chunks(k, carry):
        near_copy(k).wait_send()
        far_copy(k).wait_send()
        pass_copy(k).wait_send()
        return carry

    def drain_parts(k, carry):
        part_copy(k).wait_send()
        return carry

    lax.fori_loop(0, 2 * PIECES, drain_pieces, 0)
    lax.fori_loop(0, PIECES, drain_steps, 0)
    first_late(PIECES).wait_send()
    second_late(PIECES).wait_send()
    pair_late(PIECES, c).wait_send()
    lax.fori_loop(0, chunks, drain_chunks, 0)
    lax.fori_loop(0, half_chunks, drain_parts, 0)


def relay_device(pipe_size, section_in, norm_gain, w_query, key_value_weight, w_out):
    _, half, width = section_in.shape
    kv_cols = key_value_weight.shape[2] * key_value_weight.shape[3]
    head = key_value_weight.shape[3] // 2
    q_cols = w_query.shape[2] // 4
    freqs = np.float32(rope_base) ** (-(np.arange(head // 2).astype(np.float32) * 2.0) / head)
    angle = np.arange(2 * half).astype(np.float32)[:, None] * freqs.astype(np.float32)[None, :]
    cosine, sine = np.cos(angle), np.sin(angle)
    cosine = jnp.asarray(np.concatenate([cosine, cosine], axis=1))
    sine = jnp.asarray(np.concatenate([-sine, sine], axis=1))
    rows = half // PIECES
    steps = PIECES + 1
    message = q_cols + 2 * head
    chunks = 2 * half // ATT_ROWS
    vmem = pl.BlockSpec(memory_space=pltpu.VMEM)
    anywhere = pl.BlockSpec(memory_space=pl.ANY)
    dma = pltpu.SemaphoreType.DMA
    return pl.pallas_call(
        functools.partial(relay_kernel, pipe_size),
        out_shape=jax.ShapeDtypeStruct((1, half, width), BF16),
        in_specs=[anywhere, vmem, anywhere, anywhere, anywhere, anywhere, anywhere],
        out_specs=vmem,
        scratch_shapes=[
            pltpu.VMEM((2 * half, head), F32),
            pltpu.VMEM((2 * half, head), F32),
            pltpu.VMEM((2, half, width), BF16),
            pltpu.VMEM((4, width, q_cols + head), BF16),
            pltpu.VMEM((4 * q_cols, width), BF16),
            pltpu.VMEM((2 * rows, width), BF16),
            pltpu.VMEM((2 * rows, head), F32),
            pltpu.VMEM((steps, 2, 2 * rows, message), BF16),
            pltpu.VMEM((steps, 2, 2 * rows, message), BF16),
            pltpu.VMEM((2, 2, 2 * rows, message), F32),
            pltpu.VMEM((steps, 2 * rows, message), BF16),
            pltpu.VMEM((steps, 2 * rows, message), BF16),
            pltpu.VMEM((2, 2 * rows, message), F32),
            pltpu.VMEM((2 * half, q_cols), BF16),
            pltpu.VMEM((2, steps, 2 * rows, head), BF16),
            pltpu.VMEM((2 * half, head), BF16),
            pltpu.VMEM((2 * half, head), BF16),
            pltpu.VMEM((chunks, ATT_ROWS, 4 * q_cols), BF16),
            pltpu.VMEM((chunks // 2, ATT_ROWS, width), BF16),
            pltpu.VMEM((chunks // 2, ATT_ROWS, width), BF16),
            pltpu.VMEM((chunks // 2, ATT_ROWS, width), F32),
            dma((11,)),
            dma((2, 2 * PIECES)),
            dma((2, 2 * PIECES)),
            dma((2, steps)),
            dma((2, steps)),
            dma((2, steps)),
            dma((2, chunks)),
            dma((2, chunks)),
            dma((2, chunks)),
            dma((2, chunks // 2)),
        ],
        compiler_params=pltpu.CompilerParams(
            collective_id=0, has_side_effects=True, vmem_limit_bytes=54 * 1024 * 1024
        ),
    )(
        section_in,
        norm_gain,
        w_query[0],
        key_value_weight[0].reshape(width, kv_cols),
        w_out[0],
        cosine,
        sine,
    )


def solution(mesh):
    fits = mesh.shape["dp"] == 4 and mesh.shape["tensor"] == 2 and mesh.shape["pipe"] > 2
    body = functools.partial(relay_device, mesh.shape["pipe"]) if fits else per_device
    return jax.shard_map(
        body,
        mesh=mesh,
        in_specs=(
            P("pipe", "tensor", "dp"),
            P("pipe", "dp"),
            P("pipe", "dp", "tensor"),
            P("pipe", "dp", "tensor", None),
            P("pipe", "tensor", "dp"),
        ),
        out_specs=P("pipe", "tensor", "dp"),
        check_vma=False,
    )
```

```python
import functools

import jax
import numpy as np
import jax.numpy as jnp
from jax import lax
from jax.experimental import pallas as pl
from jax.experimental.pallas import tpu as pltpu
from jax.sharding import PartitionSpec as P

MODEL_WIDTH = 8192
QUERY_HEAD_COUNT = 32
KEY_VALUE_HEADS = 4


eps = 1e-05
rope_base = 500000.0


def shifted(block, axis, distance):
    devices = range(lax.axis_size(axis))
    route = [((i - distance) % len(devices), i) for i in devices]
    return lax.ppermute(block, axis, route)


def rope_tables(positions, head_dim):
    half = head_dim // 2
    freqs = rope_base ** (-(jnp.arange(half).astype(jnp.float32) * 2.0) / head_dim)
    angle = positions[:, None] * freqs[None, :]
    return (jnp.cos(angle), jnp.sin(angle))


def rotate(field, cosine, sine):
    half = field.shape[-1] // 2
    first = field[..., :half]
    second = field[..., half:]
    return jnp.concatenate(
        [first * cosine - second * sine, second * cosine + first * sine], axis=-1
    )


def softmax_rows(scores, allowed):
    scores = jnp.where(allowed, scores, -jnp.inf)
    top = jnp.max(scores, axis=-1, keepdims=True)
    expo = jnp.exp(scores - top)
    return (expo / jnp.sum(expo, axis=-1, keepdims=True)).astype(jnp.bfloat16)


def per_device(section_in, norm_gain, w_query, key_value_weight, w_out):
    resident = section_in[0]
    arrived = shifted(resident, "pipe", 1)
    gathered = lax.all_gather(arrived, "tensor", axis=0, tiled=True)
    seq_len = gathered.shape[0]
    width = gathered.shape[1]
    head_dim = key_value_weight.shape[3] // 2
    pair_heads = key_value_weight.shape[2]
    query_heads = w_query.shape[2] // head_dim
    groups = lax.axis_size("dp")
    member = lax.axis_index("dp")
    head_group = QUERY_HEAD_COUNT // KEY_VALUE_HEADS
    score_scale = head_dim ** (-0.5)
    wide = gathered.astype(jnp.float32)
    square_part = jnp.sum(wide * wide, axis=1)
    normed_input = (wide * norm_gain[0][None, :]).astype(jnp.bfloat16)
    pair_terms = jnp.dot(
        normed_input,
        key_value_weight[0].reshape(width, pair_heads * 2 * head_dim),
        preferred_element_type=jnp.float32,
    )
    local_rows = seq_len // groups
    first_row = member * local_rows
    positions = jnp.arange(seq_len).astype(jnp.float32)
    cosine, sine = rope_tables(positions, head_dim)
    own_cosine = lax.dynamic_slice_in_dim(cosine, first_row, local_rows, 0)
    own_sine = lax.dynamic_slice_in_dim(sine, first_row, local_rows, 0)
    own_places = lax.dynamic_slice_in_dim(positions, first_row, local_rows, 0)
    pair_share, square_share = (
        lax.psum_scatter(pair_terms, "dp", scatter_dimension=0, tiled=True),
        lax.psum_scatter(square_part, "dp", scatter_dimension=0, tiled=True),
    )
    own_scale = lax.rsqrt(square_share / MODEL_WIDTH + eps)
    pair_share = pair_share.reshape(local_rows, pair_heads, 2 * head_dim) * own_scale[:, None, None]
    own_keys = rotate(
        pair_share[..., :head_dim], own_cosine[:, None, :], own_sine[:, None, :]
    ).astype(jnp.bfloat16)
    own_values = pair_share[..., head_dim:].astype(jnp.bfloat16)
    keys, values = (
        lax.all_gather(own_keys, "dp", axis=0, tiled=True),
        lax.all_gather(own_values, "dp", axis=0, tiled=True),
    )
    w_heads = w_out[0].reshape(query_heads, head_dim, width)
    w_flat = w_query[0]
    query_sum = lax.psum_scatter(
        jnp.dot(normed_input, w_flat, preferred_element_type=jnp.float32).astype(jnp.bfloat16),
        "dp",
        scatter_dimension=0,
        tiled=True,
    ).astype(jnp.float32)
    query = rotate(
        query_sum.reshape(local_rows, query_heads, head_dim) * own_scale[:, None, None],
        own_cosine[:, None, :],
        own_sine[:, None, :],
    ).astype(jnp.bfloat16)
    allowed = positions[None, :] <= own_places[:, None]

    def attend_group(number):
        query_group = lax.dynamic_slice_in_dim(query, number * head_group, head_group, 1)
        key_head = lax.dynamic_index_in_dim(keys, number, 1, keepdims=False)
        value_head = lax.dynamic_index_in_dim(values, number, 1, keepdims=False)
        scores = (
            jnp.einsum("rgd,sd->grs", query_group, key_head, preferred_element_type=jnp.float32)
            * score_scale
        )
        weights = softmax_rows(scores, allowed[None])
        return jnp.einsum(
            "grs,sd->grd", weights, value_head, preferred_element_type=jnp.float32
        ).astype(jnp.bfloat16)

    row_results = lax.map(attend_group, jnp.arange(pair_heads))
    row_results = row_results.reshape(query_heads, local_rows, head_dim)
    contrib = jnp.einsum(
        "hsd,hdc->sc",
        lax.all_gather(row_results, "dp", axis=1, tiled=True),
        w_heads,
        preferred_element_type=jnp.float32,
    )
    summed = lax.psum_scatter(
        contrib.astype(jnp.bfloat16), "tensor", scatter_dimension=0, tiled=True
    ).astype(jnp.float32)
    result = (arrived.astype(jnp.float32) + summed).astype(jnp.bfloat16)
    return result[None]

MESH = pl.DeviceIdType.MESH
BF16 = jnp.bfloat16
F32 = jnp.float32
PIECES = 8
ATT_ROWS = 64


def relay_kernel(
    pipe_size,
    x_hbm,
    gain_ref,
    wq_hbm,
    wkv_hbm,
    wo_hbm,
    cos_hbm,
    sin_hbm,
    out_ref,
    cos_ref,
    sin_ref,
    arrived,
    w_all,
    w_out,
    normed,
    squares,
    first_send,
    first_recv,
    keep,
    second_send,
    second_recv,
    keep_two,
    query,
    pair_buf,
    keys,
    values,
    heads,
    part_send,
    part_recv,
    own_part,
    load_sem,
    z_sem,
    x_sem,
    first_sem,
    second_sem,
    pair_sem,
    near_sem,
    far_sem,
    pass_sem,
    part_sem,
):
    p = lax.axis_index("pipe")
    t = lax.axis_index("tensor")
    d = lax.axis_index("dp")
    c = d % 2
    y = d // 2
    nxt = {"pipe": (p + 1) % pipe_size}
    prev = {"pipe": (p + pipe_size - 1) % pipe_size}
    side = {"tensor": 1 - t}
    core = {"dp": d + 1 - 2 * c}
    across = {"dp": (d + 2) % 4}
    half = arrived.shape[1]
    width = arrived.shape[2]
    rows = half // PIECES
    sub = rows // 2
    q_cols = wq_hbm.shape[1] // 4
    head = wkv_hbm.shape[1] // 4
    q_heads = q_cols // head
    steps = PIECES + 1
    chunks = 2 * half // ATT_ROWS
    half_chunks = chunks // 2

    def remote(src, dst, sem, k, where):
        return pltpu.make_async_remote_copy(
            src_ref=src,
            dst_ref=dst,
            send_sem=sem.at[0, k],
            recv_sem=sem.at[1, k],
            device_id=where,
            device_id_type=MESH,
        )

    barrier = pltpu.get_barrier_semaphore()
    for where in (nxt, prev, side, core, across):
        pl.semaphore_signal(barrier, inc=1, device_id=where, device_id_type=MESH)
    pl.semaphore_wait(barrier, 5)

    def z_copy(k):
        span = pl.ds(k * sub, sub)
        return remote(x_hbm.at[0, span], arrived.at[t, span], z_sem, k, nxt)

    def x_copy(k):
        span = pl.ds(k * sub, sub)
        return remote(arrived.at[t, span], arrived.at[t, span], x_sem, k, side)

    def x_landed(k):
        span = pl.ds(k * sub, sub)
        return remote(arrived.at[1 - t, span], arrived.at[1 - t, span], x_sem, k, side)

    late = pl.ds(rows, rows)

    def first_copy(k):
        return remote(first_send.at[k], first_recv.at[k], first_sem, k, core)

    def first_late(k):
        return remote(
            first_send.at[k, :, late], first_recv.at[k, :, late], first_sem, k, core
        )

    def second_copy(k):
        return remote(second_send.at[k], second_recv.at[k], second_sem, k, across)

    def second_late(k):
        return remote(
            second_send.at[k, late], second_recv.at[k, late], second_sem, k, across
        )

    def pair_copy(k, slot):
        return remote(pair_buf.at[slot, k], pair_buf.at[slot, k], pair_sem, k, core)

    def pair_late(k, slot):
        return remote(
            pair_buf.at[slot, k, late], pair_buf.at[slot, k, late], pair_sem, k, core
        )

    def by_step(k, whole, part, act):
        @pl.when(k < PIECES)
        def _():
            act(whole)

        @pl.when(k >= PIECES)
        def _():
            act(part)

    def block(k, owner):
        return heads.at[k, :, pl.ds(pl.multiple_of(owner * q_cols, q_cols), q_cols)]

    far_owner = (d + 2) % 4

    def near_copy(k):
        return remote(block(k, d), block(k, d), near_sem, k, core)

    def far_copy(k):
        return remote(block(k, d), block(k, d), far_sem, k, across)

    def pass_copy(k):
        return remote(block(k, far_owner), block(k, far_owner), pass_sem, k, core)

    def part_copy(k):
        return remote(part_send.at[k], part_recv.at[k], part_sem, k, side)

    def start_z(k, carry):
        z_copy(k).start()
        return carry

    lax.fori_loop(0, 2 * PIECES, start_z, 0)

    loads = []
    for b in range(4):
        loads.append(
            pltpu.make_async_copy(
                wq_hbm.at[:, b * q_cols : (b + 1) * q_cols],
                w_all.at[b, :, 0:q_cols],
                load_sem.at[2 * b],
            )
        )
        loads.append(
            pltpu.make_async_copy(
                wkv_hbm.at[:, b * head : (b + 1) * head],
                w_all.at[b, :, q_cols : q_cols + head],
                load_sem.at[2 * b + 1],
            )
        )
    loads.append(pltpu.make_async_copy(cos_hbm, cos_ref, load_sem.at[9]))
    loads.append(pltpu.make_async_copy(sin_hbm, sin_ref, load_sem.at[10]))
    out_load = pltpu.make_async_copy(wo_hbm, w_out, load_sem.at[8])
    for load in loads:
        load.start()
    out_load.start()
    z_copy(0).wait_recv()
    x_copy(0).start()
    normed[...] = jnp.zeros_like(normed)
    squares[...] = jnp.zeros_like(squares)
    for load in loads:
        load.wait()

    def prepare(side_index, piece, base):
        wide = arrived[side_index, pl.ds(piece * rows, rows), :].astype(F32)
        normed[base : base + rows, :] = (wide * gain_ref[...]).astype(BF16)
        total = wide[:, 0:head] * wide[:, 0:head]
        for k in range(1, width // head):
            cut = wide[:, k * head : (k + 1) * head]
            total = total + cut * cut
        squares[base : base + rows, :] = total

    def project(s):
        for other in range(2):
            index = 2 * other + (1 - c)
            first_send[s, other, :, 0 : q_cols + head] = jnp.dot(
                normed[...], w_all[index], preferred_element_type=F32
            ).astype(BF16)
            first_send[s, other, :, q_cols + head :] = squares[...].astype(BF16)
        by_step(s, first_copy, first_late, lambda make: make(s).start())

        @pl.when(s + 1 < PIECES)
        def _():
            z_copy(2 * s + 2).wait_recv()
            x_copy(2 * s + 2).start()

        for other in range(2):
            index = 2 * other + c
            keep[s % 2, other, :, 0 : q_cols + head] = jnp.dot(
                normed[...], w_all[index], preferred_element_type=F32
            )
            keep[s % 2, other, :, q_cols + head :] = squares[...]

    def reduce_core(s):
        by_step(s, first_copy, first_late, lambda make: make(s).wait_recv())
        second_send[s] = (keep[s % 2, 1 - y] + first_recv[s, 1 - y].astype(F32)).astype(BF16)
        by_step(s, second_copy, second_late, lambda make: make(s).start())
        keep_two[s % 2] = keep[s % 2, y] + first_recv[s, y].astype(F32)

    is_value = c.astype(F32)

    def finish(s):
        by_step(s, second_copy, second_late, lambda make: make(s).wait_recv())
        total = keep_two[s % 2] + second_recv[s].astype(F32)
        scale = lax.rsqrt(
            jnp.sum(total[:, q_cols + head :], axis=1, keepdims=True) / MODEL_WIDTH + eps
        )
        own_rows = pl.ds(pl.multiple_of(t * half + (s % PIECES) * rows, rows), rows)
        side_rows = pl.ds(
            pl.multiple_of((1 - t) * half + ((s + PIECES - 1) % PIECES) * rows, rows), rows
        )
        cosine = jnp.concatenate([cos_ref[own_rows, :], cos_ref[side_rows, :]], axis=0)
        sine = jnp.concatenate([sin_ref[own_rows, :], sin_ref[side_rows, :]], axis=0)
        turned = []
        for k in range(q_heads):
            v = total[:, k * head : (k + 1) * head] * scale
            turned.append((v * cosine + pltpu.roll(v, head // 2, 1) * sine).astype(BF16))

        @pl.when(s < PIECES)
        def _():
            for k in range(q_heads):
                query[own_rows, k * head : (k + 1) * head] = turned[k][:rows]

        @pl.when(s > 0)
        def _():
            for k in range(q_heads):
                query[side_rows, k * head : (k + 1) * head] = turned[k][rows:]

        v = total[:, q_cols : q_cols + head] * scale
        pair_cos = cosine * (1.0 - is_value) + is_value
        pair_sin = sine * (1.0 - is_value)
        pair_buf[c, s] = (v * pair_cos + pltpu.roll(v, head // 2, 1) * pair_sin).astype(BF16)
        by_step(s, pair_copy, pair_late, lambda make: make(s, c).start())

    def step(s, carry):
        @pl.when(s < PIECES)
        def _():
            z_copy(2 * s + 1).wait_recv()
            x_copy(2 * s + 1).start()
            prepare(t, s, 0)

        @pl.when((s > 0) & (s < steps))
        def _():
            x_landed(2 * s - 2).wait_recv()
            x_landed(2 * s - 1).wait_recv()
            prepare(1 - t, s - 1, rows)

        @pl.when(s < steps)
        def _():
            project(s)

        @pl.when((s > 0) & (s < steps + 1))
        def _():
            reduce_core(s - 1)

        @pl.when(s > 1)
        def _():
            finish(s - 2)

        return carry

    lax.fori_loop(0, steps + 2, step, 0)

    def land_pairs(k, carry):
        pair_copy(k, 1 - c).wait_recv()
        return carry

    lax.fori_loop(0, PIECES, land_pairs, 0)
    pair_late(PIECES, 1 - c).wait_recv()

    def place(k, carry):
        own = pl.ds(pl.multiple_of(t * half + k * rows, rows), rows)
        other = pl.ds(pl.multiple_of((1 - t) * half + k * rows, rows), rows)
        keys[own, :] = pair_buf[0, k, 0:rows, :]
        keys[other, :] = pair_buf[0, k + 1, rows:, :]
        values[own, :] = pair_buf[1, k, 0:rows, :]
        values[other, :] = pair_buf[1, k + 1, rows:, :]
        return carry

    lax.fori_loop(0, PIECES, place, 0)
    out_load.wait()
    factor = head ** (-0.5) * 1.4426950408889634

    def attend(i, first, count):
        at = lax.broadcasted_iota(jnp.int32, (ATT_ROWS, count), 0) + first
        seen = lax.broadcasted_iota(jnp.int32, (ATT_ROWS, count), 1) <= at
        for k in range(q_heads):
            q = query[pl.ds(first, ATT_ROWS), k * head : (k + 1) * head]
            scores = lax.dot_general(
                q, keys[0:count, :], (((1,), (1,)), ((), ())), preferred_element_type=F32
            )
            scores = jnp.where(seen, scores, -1e30)
            top = jnp.max(scores, axis=1, keepdims=True)
            expo = jnp.exp2((scores - top) * factor)
            total = jnp.sum(expo, axis=1, keepdims=True)
            mixed = jnp.dot(expo.astype(BF16), values[0:count, :], preferred_element_type=F32)
            spot = pl.ds(pl.multiple_of(d * q_cols + k * head, head), head)
            heads[i, :, spot] = (mixed / total).astype(BF16)

    def out_step(i, carry):
        @pl.when(i < chunks)
        def _():
            which = (1 - t + i // half_chunks) % 2
            first = pl.multiple_of(which * half + (i % half_chunks) * ATT_ROWS, ATT_ROWS)

            @pl.when(which == 0)
            def _():
                attend(i, first, half)

            @pl.when(which == 1)
            def _():
                attend(i, first, 2 * half)

            far_copy(i).start()
            near_copy(i).start()

        @pl.when((i > 0) & (i < chunks + 1))
        def _():
            far_landed(i - 1).wait_recv()
            pass_copy(i - 1).start()

        @pl.when(i > 1)
        def _():
            k = i - 2
            near_landed(k).wait_recv()
            pass_landed(k).wait_recv()

            @pl.when(k < half_chunks)
            def _():
                for n in range(4):
                    cut = slice(n * (width // 4), (n + 1) * (width // 4))
                    part_send[k, :, cut] = jnp.dot(
                        heads[k], w_out[:, cut], preferred_element_type=F32
                    ).astype(BF16)
                part_copy(k).start()

            @pl.when((k >= half_chunks) & (k % 2 == 1))
            def _():
                both = heads[pl.ds(k - 1, 2)].reshape(2 * ATT_ROWS, 4 * q_cols)
                for n in range(4):
                    cut = slice(n * (width // 4), (n + 1) * (width // 4))
                    own_part[pl.ds(k - half_chunks - 1, 2), :, cut] = jnp.dot(
                        both, w_out[:, cut], preferred_element_type=F32
                    ).reshape(2, ATT_ROWS, width // 4)

        return carry

    def far_landed(k):
        return remote(block(k, far_owner), block(k, far_owner), far_sem, k, across)

    def near_landed(k):
        owner = d + 1 - 2 * c
        return remote(block(k, owner), block(k, owner), near_sem, k, core)

    def pass_landed(k):
        owner = (d + 3 - 2 * c) % 4
        return remote(block(k, owner), block(k, owner), pass_sem, k, core)

    lax.fori_loop(0, chunks + 2, out_step, 0)

    def close(k, carry):
        part_copy(k).wait_recv()
        span = pl.ds(pl.multiple_of(k * ATT_ROWS, ATT_ROWS), ATT_ROWS)
        out_ref[0, span, :] = (
            arrived[t, span, :].astype(F32) + (own_part[k] + part_recv[k].astype(F32))
        ).astype(BF16)
        return carry

    lax.fori_loop(0, half_chunks, close, 0)

    def drain_pieces(k, carry):
        z_copy(k).wait_send()
        x_copy(k).wait_send()
        return carry

    def drain_steps(k, carry):
        first_copy(k).wait_send()
        second_copy(k).wait_send()
        pair_copy(k, c).wait_send()
        return carry

    def drain_chunks(k, carry):
        near_copy(k).wait_send()
        far_copy(k).wait_send()
        pass_copy(k).wait_send()
        return carry

    def drain_parts(k, carry):
        part_copy(k).wait_send()
        return carry

    lax.fori_loop(0, 2 * PIECES, drain_pieces, 0)
    lax.fori_loop(0, PIECES, drain_steps, 0)
    first_late(PIECES).wait_send()
    second_late(PIECES).wait_send()
    pair_late(PIECES, c).wait_send()
    lax.fori_loop(0, chunks, drain_chunks, 0)
    lax.fori_loop(0, half_chunks, drain_parts, 0)


def relay_device(pipe_size, section_in, norm_gain, w_query, key_value_weight, w_out):
    _, half, width = section_in.shape
    kv_cols = key_value_weight.shape[2] * key_value_weight.shape[3]
    head = key_value_weight.shape[3] // 2
    q_cols = w_query.shape[2] // 4
    freqs = np.float32(rope_base) ** (-(np.arange(head // 2).astype(np.float32) * 2.0) / head)
    angle = np.arange(2 * half).astype(np.float32)[:, None] * freqs.astype(np.float32)[None, :]
    cosine, sine = np.cos(angle), np.sin(angle)
    cosine = jnp.asarray(np.concatenate([cosine, cosine], axis=1))
    sine = jnp.asarray(np.concatenate([-sine, sine], axis=1))
    rows = half // PIECES
    steps = PIECES + 1
    message = q_cols + 2 * head
    chunks = 2 * half // ATT_ROWS
    vmem = pl.BlockSpec(memory_space=pltpu.VMEM)
    anywhere = pl.BlockSpec(memory_space=pl.ANY)
    dma = pltpu.SemaphoreType.DMA
    return pl.pallas_call(
        functools.partial(relay_kernel, pipe_size),
        out_shape=jax.ShapeDtypeStruct((1, half, width), BF16),
        in_specs=[anywhere, vmem, anywhere, anywhere, anywhere, anywhere, anywhere],
        out_specs=vmem,
        scratch_shapes=[
            pltpu.VMEM((2 * half, head), F32),
            pltpu.VMEM((2 * half, head), F32),
            pltpu.VMEM((2, half, width), BF16),
            pltpu.VMEM((4, width, q_cols + head), BF16),
            pltpu.VMEM((4 * q_cols, width), BF16),
            pltpu.VMEM((2 * rows, width), BF16),
            pltpu.VMEM((2 * rows, head), F32),
            pltpu.VMEM((steps, 2, 2 * rows, message), BF16),
            pltpu.VMEM((steps, 2, 2 * rows, message), BF16),
            pltpu.VMEM((2, 2, 2 * rows, message), F32),
            pltpu.VMEM((steps, 2 * rows, message), BF16),
            pltpu.VMEM((steps, 2 * rows, message), BF16),
            pltpu.VMEM((2, 2 * rows, message), F32),
            pltpu.VMEM((2 * half, q_cols), BF16),
            pltpu.VMEM((2, steps, 2 * rows, head), BF16),
            pltpu.VMEM((2 * half, head), BF16),
            pltpu.VMEM((2 * half, head), BF16),
            pltpu.VMEM((chunks, ATT_ROWS, 4 * q_cols), BF16),
            pltpu.VMEM((chunks // 2, ATT_ROWS, width), BF16),
            pltpu.VMEM((chunks // 2, ATT_ROWS, width), BF16),
            pltpu.VMEM((chunks // 2, ATT_ROWS, width), F32),
            dma((11,)),
            dma((2, 2 * PIECES)),
            dma((2, 2 * PIECES)),
            dma((2, steps)),
            dma((2, steps)),
            dma((2, steps)),
            dma((2, chunks)),
            dma((2, chunks)),
            dma((2, chunks)),
            dma((2, chunks // 2)),
        ],
        compiler_params=pltpu.CompilerParams(
            collective_id=0, has_side_effects=True, vmem_limit_bytes=54 * 1024 * 1024
        ),
    )(
        section_in,
        norm_gain,
        w_query[0],
        key_value_weight[0].reshape(width, kv_cols),
        w_out[0],
        cosine,
        sine,
    )


def solution(mesh):
    fits = mesh.shape["dp"] == 4 and mesh.shape["tensor"] == 2 and mesh.shape["pipe"] > 2
    body = functools.partial(relay_device, mesh.shape["pipe"]) if fits else per_device
    return jax.shard_map(
        body,
        mesh=mesh,
        in_specs=(
            P("pipe", "tensor", "dp"),
            P("pipe", "dp"),
            P("pipe", "dp", "tensor"),
            P("pipe", "dp", "tensor", None),
            P("pipe", "tensor", "dp"),
        ),
        out_specs=P("pipe", "tensor", "dp"),
        check_vma=False,
    )
```
